256 devices in a mesh: tp: 32 (over x, z), dp: 8 (over y, core).
Axes of the slice: x: 4, y: 4, z: 8, core: 2. Of those that a mesh axis runs over, the one named last changes fastest.
Arguments:
- hidden: bfloat16 [32768, 1600], P(('dp', 'tp')), parts along dimension 0
- gain: bfloat16 [1600], replicated, may hold values from 0.5 to 1.5
- head: bfloat16 [1600, 32000], P(None, 'tp')
- lengths: int32 [128], P('dp'), parts along dimension 0, may hold values from 64 to 256, as said below
- mask: int32 [32768], P(('dp', 'tp')), parts along dimension 0, may hold values 0 or 1
- targets: int32 [32768], P(('dp', 'tp')), parts along dimension 0, may hold values from 0 to 31999
Outputs:
- logprob: float32 [32768], P(('dp', 'tp')), parts along dimension 0
- entropy: float32 [32768], P(('dp', 'tp')), parts along dimension 0
The draws below stay inside these ranges and needn't reach their ends.
There are 8 independent parts, one for each index of `dp`. The reference program is written for one: setup_inputs(seed, part) draws one part's arguments, and reference() takes and returns one part's arrays. A program takes and returns all parts, laid end to end along the dimension named above; an argument that names none is the same for every part. Nothing has to cross between parts.
Inputs may be any that keep to these rules, and one draw needn't show every extreme that they name: `lengths`: each sequence's live length; the longest sequence of a batch fills all 256 slots.
All inputs are finite; a program needn't handle non-finite values. No bound on the sum of `mask` on one device may be relied on, other than what follows from the above.
Results may differ from the reference program's by a relative error of at most 0.003.
The reference program's roundings to bfloat16 on the way (of `normed`) count: a program that leaves them out, or rounds other values in their place, can miss the bound.
Values may be sent and summed in bfloat16 or wider, within the bound.
A program may use at most 128 MiB of HBM per device.

```python
import math
import jax
import jax.numpy as jnp
import numpy as np
from jax import lax

D = 1600
VOCAB = 32000
SEQ_LEN = 256
TOKENS = 4096
SEQS = 16


def draw_hidden(key, part):
    k_base, k_rows, k_cols = jax.random.split(jax.random.fold_in(key, 11), 3)
    row_scale = jnp.exp(jax.random.uniform(k_rows, (TOKENS, 1), jnp.float32) * math.log(10.0))
    col_scale = jnp.exp(jax.random.uniform(k_cols, (1, D), jnp.float32) * math.log(10.0))
    base = jax.random.normal(k_base, (TOKENS, D), jnp.float32)
    values = base * row_scale * col_scale
    return values.astype(jnp.bfloat16)


def draw_head(key, part):
    k_base, k_cols = jax.random.split(jax.random.fold_in(key, 23), 2)
    cols = jnp.arange(VOCAB).astype(jnp.float32)
    col_scale = jnp.exp(jax.random.uniform(k_cols, (1, VOCAB), jnp.float32) * math.log(6.0)) * (1.0 + 2.0 * cols / VOCAB)[None, :]
    base = jax.random.normal(k_base, (D, VOCAB), jnp.float32)
    values = base * col_scale / jnp.sqrt(D * 1.0)
    return values.astype(jnp.bfloat16)


def draw_lengths(key, part):
    k_len, k_full = jax.random.split(jax.random.fold_in(key, 37))
    drawn = jax.random.randint(k_len, (SEQS,), SEQ_LEN // 4, SEQ_LEN + 1)
    full_at = jax.random.randint(k_full, (), 0, SEQS)
    return jnp.where(jnp.arange(SEQS) == full_at, SEQ_LEN, drawn).astype(jnp.int32)


def plant(entries, key, low, largest):
    shape = entries.shape
    index_at = [jax.random.randint(jax.random.fold_in(key, axis), (), 0, shape[axis]) for axis in range(len(shape))]
    entries = entries.at[tuple(index_at)].set(low)
    longest = shape.index(max(shape))
    index_at[longest] = (index_at[longest] + 1) % shape[longest]
    return entries.at[tuple(index_at)].set(largest)


def rank_table(number_of, skew):
    loads = [(1 << 20) // math.isqrt(grade ** skew) + 1 for grade in range(1, number_of + 1)]
    spread = 1 + sum(loads) // (1 << 30)
    return np.cumsum(np.array([max(1, weight // spread) for weight in loads]))


def ranked(key, shape, count, skew):
    listing = rank_table(count, skew)
    ticket = jax.random.randint(jax.random.fold_in(key, 1), shape, 0, int(listing[count - 1]))
    rank = jnp.searchsorted(jnp.asarray(listing, jnp.int32), ticket, side="right")
    return jax.random.permutation(jax.random.fold_in(key, 2), count)[rank].astype(jnp.int32)


def setup_inputs(seed: int = 0, part: int = 0) -> dict:
    key_list = jax.random.split(jax.random.key(seed), 7)
    part_splits = jax.random.split(jax.random.fold_in(key_list[6], part), 7)
    return {
        "hidden": draw_hidden(jax.random.fold_in(jax.random.fold_in(key_list[6], part), 71), part),
        "gain": jnp.clip(1.0 + 0.1 * jax.random.normal(key_list[1], (D,), jnp.float32), 0.5, 1.5).astype(jnp.bfloat16),
        "head": draw_head(jax.random.fold_in(key_list[6], 71), part),
        "lengths": draw_lengths(jax.random.fold_in(jax.random.fold_in(key_list[6], part), 71), part),
        "mask": plant((jax.random.randint(part_splits[4], (TOKENS,), 0, 4) < 3).astype(jnp.int32), jax.random.fold_in(part_splits[4], 1), 0, 1),
        "targets": plant(ranked(part_splits[5], (TOKENS,), VOCAB, 1), jax.random.fold_in(part_splits[5], 3), 0, VOCAB - 1).astype(jnp.int32),
    }


EPS = 1e-06

def reference(hidden, gain, head, lengths, mask, targets):
    xf = hidden.astype(jnp.float32)
    meansq = lax.optimization_barrier(jnp.mean(xf * xf, axis=-1, keepdims=True))
    normed = (xf * lax.rsqrt(meansq + EPS) * gain.astype(jnp.float32)).astype(jnp.bfloat16)
    headf = head.astype(jnp.float32)
    blocks = TOKENS // SEQ_LEN
    rows_b = normed.reshape(blocks, SEQ_LEN, D)
    tgt_b = targets.reshape(blocks, SEQ_LEN)

    def one_block(item):
        rows, tgt = item
        logits = jnp.dot(rows.astype(jnp.float32), headf)
        top = lax.optimization_barrier(jnp.max(logits, axis=-1))
        shifted = logits - top[:, None]
        expo = jnp.exp(shifted)
        total = lax.optimization_barrier(jnp.sum(expo, axis=-1))
        lse = top + jnp.log(total)
        picked = jnp.take_along_axis(logits, tgt[:, None].astype(jnp.int32), axis=1)[:, 0]
        logp = picked - lse
        ent = jnp.log(total) - lax.optimization_barrier(jnp.sum(expo * shifted, axis=-1)) / total
        return (logp, ent)
    logp, ent = lax.map(one_block, (rows_b, tgt_b))
    logp = logp.reshape(TOKENS)
    ent = ent.reshape(TOKENS)
    row_ids = jnp.arange(TOKENS, dtype=jnp.int32)
    slot = row_ids % SEQ_LEN
    seq_id = row_ids // SEQ_LEN
    seq_len = lengths.astype(jnp.int32)[seq_id]
    valid = (slot < seq_len) & (mask == 1)
    zero = jnp.zeros_like(logp)
    return (jnp.where(valid, logp, zero), jnp.where(valid, ent, zero))
```

```python
import functools

import jax
import jax.numpy as jnp
from jax import lax
from jax.experimental import pallas as pl
from jax.experimental.pallas import tpu as pltpu
from jax.sharding import PartitionSpec as P

SEQ_LEN = 256
EPS = 1e-06

NX, NY, NZ = 4, 4, 8
D = 1600
DE = 1664
ROWS = 128
WIDTH = 1000
TILES = 8
LAST = WIDTH - 7 * 128
SUB = D // 2
HALF = ROWS // 2
GROUP = 256
MESH = pl.DeviceIdType.MESH

PLACE = {1: 0, 7: 1, 2: 2, 6: 3, 3: 4, 5: 5, 0: 6, 4: 7}

X_SEQ = (
    ((1, 0, 0), (1, 0, 1), (1, 1, 0), (1, 1, 1), (3, 0, 0), (3, 0, 1)),
    ((2, 1, 0), (2, 1, 1), (2, 0, 0), (2, 0, 1), (3, 1, 0), (3, 1, 1)),
)
Y_SEQ = (
    ((1, 0, 0), (1, 0, 1), (2, 0, 0), (2, 0, 1), (3, 0, 0), (3, 0, 1)),
    ((2, 1, 0), (2, 1, 1), (1, 1, 0), (1, 1, 1), (3, 1, 0), (3, 1, 1)),
)
Z_SEQ = (
    ((1, 0), (1, 1), (2, 0), (2, 1), (3, 0), (3, 1), (4, 0)),
    ((7, 0), (7, 1), (6, 0), (6, 1), (5, 0), (5, 1), (4, 1)),
)


def unit_of(n, h):
    p = jnp.where(n < 4, -1, (n - 4) // 2)
    u = jnp.where(n < 4, n, (n - 4) % 2)
    other = 1 - h
    shard = jnp.where(p < 0, 0, jnp.where((p == 3) | (p == 5), 3, jnp.where(p == 4, 2 - u, 1 + u)))
    mine = (p == 0) | (p == 1) | (p == 3)
    low = jnp.where(p == 1, 1 - u, u)
    k = jnp.where(p < 0, u, 2 * jnp.where(mine, h, other) + low)
    return shard, k


def compute_step(tok, hb, tb, mx, sm, en, tg, row0, shard, k, col0, first):
    row0 = pl.multiple_of(row0, GROUP)
    rows = pl.ds(row0, GROUP)
    left = tok[rows, :D]
    right = jnp.concatenate([hb[shard, 2 * k], hb[shard, 2 * k + 1]], axis=1)
    logits = jnp.dot(left, right, preferred_element_type=jnp.float32)
    l0, l1 = logits[:, :128], logits[:, 128:]
    lane = lax.broadcasted_iota(jnp.int32, (GROUP, 128), 1)
    inside = lane < jnp.where(k == 3, LAST, 128)
    aim = tb[rows, :]
    base = col0.astype(jnp.float32)
    t = tg[rows, :]
    t = jnp.where(aim == base, l0, t)
    t = jnp.where((aim == base + 128.0) & inside, l1, t)
    tg[rows, :] = t
    l1 = jnp.where(inside, l1, l0)
    old = jnp.where(first, l0, mx[rows, :])
    new = jnp.maximum(jnp.maximum(l0, l1), old)
    d0, d1, da = l0 - new, l1 - new, old - new
    e0, e1, a = jnp.exp(d0), jnp.where(inside, jnp.exp(d1), 0.0), jnp.exp(da)
    s = sm[rows, :]
    en[rows, :] = (en[rows, :] + da * s) * a + (e0 * d0 + e1 * d1)
    sm[rows, :] = s * a + (e0 + e1)
    mx[rows, :] = new


def aim_rows(tok, tb, row0, count):
    ids = tok[pl.ds(row0, count), pl.ds(D, DE - D)].astype(jnp.float32)
    value = ids[:, 0:1] * 256.0 + ids[:, 1:2]
    lane = lax.broadcasted_iota(jnp.int32, (count, 128), 1).astype(jnp.float32)
    tb[pl.ds(row0, count), :] = value - lane


def block_stats(mx, sm, en, tg, row0):
    rows = pl.ds(row0, ROWS)
    m, s, e = mx[rows, :].T, sm[rows, :].T, en[rows, :].T
    top = jnp.max(m, axis=0, keepdims=True)
    gap = m - top
    scale = jnp.exp(gap)
    total = jnp.sum(s * scale, axis=0, keepdims=True)
    ent = jnp.sum((e + gap * s) * scale, axis=0, keepdims=True)
    tgt = jnp.sum(tg[rows, :].T, axis=0, keepdims=True)
    return top, total, ent, tgt


def kernel(
    rows_ref, head_ref, tail_ref, out_ref,
    tok, hb, tb, mx, sm, en, tg, stats, sendbuf, inbox,
    load_sem, xs, xr, ys, yr, zs, zr, bs, br, ss, sr,
):
    tp, dp = lax.axis_index("tp"), lax.axis_index("dp")
    x, z = tp // NZ, tp % NZ
    y, core = dp // 2, dp % 2
    h = y % 2

    def x_peer(step):
        return {"tp": ((x + step) % NX) * NZ + z, "dp": dp}

    def y_peer(step):
        return {"tp": tp, "dp": ((y + step) % NY) * 2 + core}

    def z_peer(step):
        return {"tp": x * NZ + (z + step) % NZ, "dp": dp}

    twin = {"tp": tp, "dp": y * 2 + 1 - core}

    def remote(src, dst, send, recv, peer):
        return pltpu.make_async_remote_copy(
            src_ref=src, dst_ref=dst, send_sem=send, recv_sem=recv, device_id=peer, device_id_type=MESH
        )

    own = PLACE[0] * ROWS
    loads = [pltpu.make_async_copy(rows_ref, tok.at[pl.ds(own, ROWS), :], load_sem.at[8])]
    for t in range(TILES - 1):
        loads.append(pltpu.make_async_copy(head_ref.at[:, pl.ds(t * 128, 128)], hb.at[0, t], load_sem.at[t]))
    loads.append(pltpu.make_async_copy(tail_ref, hb.at[0, TILES - 1], load_sem.at[7]))
    for copy in loads:
        copy.start()

    barrier = pltpu.get_barrier_semaphore()
    peers = [x_peer(1), x_peer(-1), y_peer(1), y_peer(-1), twin] + [z_peer(d) for d in range(1, NZ)]
    for peer in peers:
        pl.semaphore_signal(barrier, inc=1, device_id=peer, device_id_type=MESH)
    pl.semaphore_wait(barrier, len(peers))

    sent = []

    def go(copy):
        copy.start()
        sent.append(copy)

    def piece(shard, tile, sub):
        return hb.at[shard, tile, pl.ds(sub * SUB, SUB), :]

    def place(d, half):
        return tok.at[pl.ds(PLACE[d] * ROWS + half * HALF, HALF), :]

    def tile_of(parity, quarter):
        return (2 * parity + quarter) * 2 + core

    def x_copy(side, i, src_shard):
        shard, quarter, sub = X_SEQ[side][i]
        tile = tile_of(h, quarter)
        return remote(
            piece(src_shard, tile, sub), piece(shard, tile, sub), xs.at[side, i], xr.at[side, i],
            x_peer(-1 if side == 0 else 1),
        )

    def y_copy(side, i, parity):
        shard, quarter, sub = Y_SEQ[side][i]
        tile = tile_of(parity, quarter)
        return remote(
            piece(shard, tile, sub), piece(shard, tile, sub), ys.at[side, i], yr.at[side, i],
            y_peer(-1 if side == 0 else 1),
        )

    def b_copy(kind, i, sender):
        shard, quarter, sub = (X_SEQ + Y_SEQ)[kind][i]
        parity = h if kind < 2 else 1 - h
        tile = (2 * parity + quarter) * 2 + sender
        return remote(piece(shard, tile, sub), piece(shard, tile, sub), bs.at[kind, i], br.at[kind, i], twin)

    def z_copy(side, i, src):
        d, half = Z_SEQ[side][i]
        return remote(
            place(src, half), place(d, half), zs.at[side, i], zr.at[side, i], z_peer(-1 if side == 0 else 1)
        )

    loads[0].wait()
    for i in range(2):
        for side in range(2):
            go(z_copy(side, i, 0))
    for copy in loads[1:]:
        copy.wait()
    for i in range(4):
        for side in range(2):
            go(x_copy(side, i, 0))

    def zero(i, carry):
        rows = pl.ds(pl.multiple_of(i * ROWS, ROWS), ROWS)
        blank = jnp.zeros((ROWS, 128), jnp.float32)
        for ref in (mx, sm, en, tg):
            ref[rows, :] = blank
        return carry

    lax.fori_loop(0, NZ, zero, 0)
    aim_rows(tok, tb, own, ROWS)

    def got_x(i):
        for side in range(2):
            shard, quarter, sub = X_SEQ[side][i]
            x_copy(side, i, 0).wait_recv()
            to = 0 if quarter == 0 else 1
            go(y_copy(to, Y_SEQ[to].index((shard, quarter, sub)), h))
            go(b_copy(side, i, core))
            if i < 2:
                go(x_copy(side, i + 4, shard))

    def got_y(i):
        for side in range(2):
            y_copy(side, i, 1 - h).wait_recv()
            go(b_copy(2 + side, i, core))

    def got_twin(kinds, i):
        for kind in kinds:
            b_copy(kind, i, 1 - core).wait_recv()

    def got_z(i):
        for side in range(2):
            d, half = Z_SEQ[side][i]
            z_copy(side, i, 0).wait_recv()
            if i + 2 < len(Z_SEQ[side]):
                if Z_SEQ[side][i + 2][1] == half:
                    go(z_copy(side, i + 2, d))
            if i == 5 and side == 1:
                go(z_copy(side, 6, d))

    def phase(g0, groups, n0, units):
        def one(i, carry):
            g, n = g0 + i // units, n0 + i % units
            shard, k = unit_of(n, h)
            step = jnp.where(shard == 2, 3, jnp.where(shard == 3, 2, shard))
            col0 = (((x + step) % NX) * NZ + z) * WIDTH + k * 256
            compute_step(tok, hb, tb, mx, sm, en, tg, g * GROUP, shard, k, col0, n == 0)
            return carry

        lax.fori_loop(0, groups * units, one, 0)

    X, Y = (0, 1), (2, 3)
    got_x(0)
    got_z(0)
    got_x(1)
    got_z(1)
    got_y(0)
    aim_rows(tok, tb, 0, GROUP)
    phase(0, 1, 0, 4)
    got_x(2)
    got_twin(X, 0)
    got_twin(X, 1)
    got_z(2)
    phase(0, 1, 4, 2)
    got_y(1)
    got_x(3)
    got_z(3)
    got_y(2)
    aim_rows(tok, tb, GROUP, GROUP)
    phase(1, 1, 0, 6)
    got_x(4)
    got_z(4)
    got_twin(X, 2)
    got_twin(X, 3)
    got_twin(Y, 0)
    got_twin(Y, 1)
    phase(0, 2, 6, 4)
    got_x(5)
    got_z(5)
    got_y(3)
    aim_rows(tok, tb, 2 * GROUP, GROUP)
    phase(2, 1, 0, 10)
    got_y(4)
    got_twin(X, 4)
    got_twin(X, 5)
    got_twin(Y, 2)
    got_twin(Y, 3)
    phase(0, 3, 10, 4)
    got_z(6)
    got_y(5)
    aim_rows(tok, tb, PLACE[4] * ROWS, ROWS)
    phase(3, 1, 0, 14)
    got_twin(Y, 4)
    got_twin(Y, 5)
    phase(0, 4, 14, 2)

    def collect(i, carry):
        parts = block_stats(mx, sm, en, tg, pl.multiple_of(i * ROWS, ROWS))
        for n, part in enumerate(parts):
            stats[i, n:n + 1, :] = part
        return carry

    lax.fori_loop(0, NZ, collect, 0)
    move = pltpu.make_async_copy(stats, sendbuf, load_sem.at[0])
    move.start()
    move.wait()
    for d in range(1, NZ):
        go(remote(sendbuf.at[PLACE[d]], inbox.at[NZ - d], ss.at[d], sr.at[NZ - d], z_peer(d)))
    for d in range(1, NZ):
        remote(sendbuf.at[PLACE[d]], inbox.at[d], ss.at[d], sr.at[d], z_peer(d)).wait_recv()
    all_of = [stats[PLACE[0]]] + [inbox[d] for d in range(1, NZ)]
    top = functools.reduce(jnp.maximum, [part[0:1, :] for part in all_of])
    total = ent = tgt = jnp.zeros((1, ROWS), jnp.float32)
    for part in all_of:
        gap = part[0:1, :] - top
        scale = jnp.exp(gap)
        total += part[1:2, :] * scale
        ent += (part[2:3, :] + gap * part[1:2, :]) * scale
        tgt += part[3:4, :]
    log_total = jnp.log(total)
    out_ref[0:1, :] = tgt - (top + log_total)
    out_ref[1:2, :] = log_total - ent / total
    for copy in sent:
        copy.wait_send()


def on_device(hidden, gain, head, lengths, mask, targets):
    rows = hidden.shape[0]
    me = lax.axis_index("tp")
    xf = hidden.astype(jnp.float32)
    meansq = jnp.mean(xf * xf, axis=-1, keepdims=True)
    normed = (xf * lax.rsqrt(meansq + EPS) * gain.astype(jnp.float32)).astype(jnp.bfloat16)
    ids = jnp.stack([targets // 256, targets % 256], axis=1).astype(jnp.bfloat16)
    wide = jnp.concatenate([normed, ids, jnp.zeros((rows, DE - D - 2), jnp.bfloat16)], axis=1)
    tail = jnp.pad(head[:, 7 * 128:], ((0, 0), (0, 128 - LAST)))
    vm = pltpu.VMEM
    dma = pltpu.SemaphoreType.DMA
    stat = vm((NZ * ROWS, 128), jnp.float32)
    small = vm((NZ, 8, 128), jnp.float32)
    out = pl.pallas_call(
        kernel,
        out_shape=jax.ShapeDtypeStruct((8, ROWS), jnp.float32),
        in_specs=[pl.BlockSpec(memory_space=pl.ANY)] * 3,
        out_specs=pl.BlockSpec(memory_space=pltpu.VMEM),
        scratch_shapes=[
            vm((NZ * ROWS, DE), jnp.bfloat16),
            vm((NX, TILES, D, 128), jnp.bfloat16),
            stat, stat, stat, stat, stat,
            small, small, small,
            dma((9,)),
            dma((2, 6)), dma((2, 6)),
            dma((2, 6)), dma((2, 6)),
            dma((2, 7)), dma((2, 7)),
            dma((4, 6)), dma((4, 6)),
            dma((NZ,)), dma((NZ,)),
        ],
        compiler_params=pltpu.CompilerParams(
            collective_id=0, has_side_effects=True, vmem_limit_bytes=48 << 20
        ),
    )(wide, head, tail)
    row_ids = me * rows + jnp.arange(rows, dtype=jnp.int32)
    slot = row_ids % SEQ_LEN
    seq_id = row_ids // SEQ_LEN
    match = seq_id[:, None] == jnp.arange(lengths.shape[0], dtype=jnp.int32)[None, :]
    seq_len = jnp.sum(jnp.where(match, lengths[None, :], 0), axis=1)
    valid = (slot < seq_len) & (mask == 1)
    return (jnp.where(valid, out[0], 0.0), jnp.where(valid, out[1], 0.0))


def solution(mesh):
    return jax.shard_map(
        on_device,
        mesh=mesh,
        in_specs=(
            P(("dp", "tp"), None),
            P(),
            P(None, "tp"),
            P("dp"),
            P(("dp", "tp")),
            P(("dp", "tp")),
        ),
        out_specs=(P(("dp", "tp")), P(("dp", "tp"))),
        check_vma=False,
    )
```

```python
import functools

import jax
import jax.numpy as jnp
from jax import lax
from jax.experimental import pallas as pl
from jax.experimental.pallas import tpu as pltpu
from jax.sharding import PartitionSpec as P

SEQ_LEN = 256
EPS = 1e-06

NX, NY, NZ = 4, 4, 8
D = 1600
DE = 1664
ROWS = 128
WIDTH = 1000
TILES = 8
LAST = WIDTH - 7 * 128
SUBS = 4
SUB = D // SUBS
HALF = ROWS // 2
MESH = pl.DeviceIdType.MESH

PLACE = {1: 0, 7: 1, 2: 2, 6: 3, 3: 4, 5: 5, 0: 6, 4: 7}

X_SEQ = tuple(
    tuple((shard, quarter, sub) for shard, quarter in seq for sub in range(SUBS))
    for seq in (((1, 0), (1, 1), (3, 0)), ((2, 1), (2, 0), (3, 1)))
)
Y_SEQ = tuple(
    tuple((shard, quarter, sub) for shard, quarter in seq for sub in range(SUBS))
    for seq in (((1, 0), (2, 0), (3, 0)), ((2, 1), (1, 1), (3, 1)))
)
Z_SEQ = (
    ((1, 0), (1, 1), (2, 0), (2, 1), (3, 0), (3, 1), (4, 0)),
    ((7, 0), (7, 1), (6, 0), (6, 1), (5, 0), (5, 1), (4, 1)),
)

QUADS = ((0, 1), (2, 4), (3, 6), (5, 7))
STEPS = (
    ("A", 0, 0), ("A", 1, 0), ("A", 2, 0), ("B", 0, 2), ("B", 0, 4), ("A", 3, 0), ("A", 0, 1), ("A", 3, 1),
    ("A", 4, 0), ("A", 4, 1), ("B", 0, 3), ("B", 1, 3), ("B", 0, 6), ("B", 1, 6), ("A", 5, 0), ("A", 5, 1),
    ("A", 0, 2), ("A", 5, 2), ("B", 0, 5), ("B", 1, 5), ("A", 6, 0), ("A", 6, 1), ("A", 6, 2), ("B", 2, 5),
    ("A", 7, 0), ("A", 7, 1), ("A", 7, 2), ("A", 7, 3), ("B", 2, 7), ("B", 1, 7), ("B", 0, 7), ("A", 0, 3),
)
DONE = {27: (7,), 28: (4, 5), 29: (2, 3), 30: (0, 1)}

TIMES = {"x0": 5.0, "x": 2.22, "z0": 5.5, "z": 4.63, "y": 4.2, "twin": 1.5, "step": 0.81}


def needs(step):
    kind, rows, columns = step
    tokens = rows if kind == "A" else 2 * rows + 2
    wanted = [("z", i) for i in range(tokens)]
    for p in QUADS[columns] if kind == "A" else (columns,):
        if p in (2, 3, 5):
            upto = SUBS * ((2, 3, 5).index(p) + 1)
            wanted += [(s, i) for s in ("x", "tx") for i in range(upto)]
        if p in (4, 6, 7):
            upto = SUBS * ((4, 6, 7).index(p) + 1)
            wanted += [(s, i) for s in ("y", "ty") for i in range(upto)]
    return set(wanted)


def plan():
    at = {}
    for i in range(3 * SUBS):
        at["x", i] = TIMES["x0"] + TIMES["x"] * (i + 1)
        at["y", i] = at["x", i] + TIMES["y"]
        at["tx", i] = at["x", i] + TIMES["twin"]
        at["ty", i] = at["y", i] + TIMES["twin"]
    for i in range(7):
        at["z", i] = TIMES["z0"] + TIMES["z"] * (i + 1)
    left = sorted(at, key=lambda event: (at[event], event))
    now, ahead = TIMES["x0"], []
    for step in STEPS:
        wanted, events = needs(step), []
        while left and (at[left[0]] <= now or wanted & set(left)):
            event = left.pop(0)
            now = max(now, at[event])
            events.append(event)
        ahead.append(events)
        now += TIMES["step"]
    return ahead, left


def packed(i):
    codes = [(0 if kind == "A" else 64) + rows * 8 + columns for kind, rows, columns in STEPS]
    words = [sum(code << (7 * j) for j, code in enumerate(codes[w:w + 4])) for w in range(0, len(codes), 4)]
    word = jnp.int32(words[0])
    for w in range(1, len(words)):
        word = jnp.where(i // 4 == w, jnp.int32(words[w]), word)
    shift = 7 * (i % 4)
    code = lax.shift_right_logical(word, shift) & 127
    return code // 64, (code // 8) % 8, code % 8


def pair_units(p, h):
    mine = (p == 2) | (p == 3) | (p == 5)
    half = jnp.where(mine, h, 1 - h)
    units = []
    for u in range(2):
        crossed = jnp.where(p == 6, 2 - u, 1 + u)
        shard = jnp.where(p < 2, 0, jnp.where((p == 5) | (p == 7), 3, crossed))
        low = jnp.where(p == 3, 1 - u, u)
        units.append((shard, jnp.where(p < 2, 2 * p + u, 2 * half + low)))
    return units


def compute_step(tok, hb, tb, mx, sm, en, tg, spans, units, first):
    def load(ref):
        return jnp.concatenate([ref[rows, :] for rows in spans], axis=0)

    def store(ref, value):
        at = 0
        for rows in spans:
            ref[rows, :] = value[at:at + rows.size, :]
            at += rows.size

    left = jnp.concatenate([tok[rows, :D] for rows in spans], axis=0)
    tiles = [hb[shard, 2 * k + j] for shard, k, _ in units for j in range(2)]
    logits = jnp.dot(left, jnp.concatenate(tiles, axis=1), preferred_element_type=jnp.float32)
    parts = [logits[:, i * 128:(i + 1) * 128] for i in range(len(tiles))]
    lane = lax.broadcasted_iota(jnp.int32, (left.shape[0], 128), 1)
    aim, t = load(tb), load(tg)
    inside = []
    for i, (_, k, col0) in enumerate(units):
        base = col0.astype(jnp.float32)
        within = lane < jnp.where(k == 3, LAST, 128)
        inside += [None, within]
        t = jnp.where(aim == base, parts[2 * i], t)
        t = jnp.where((aim == base + 128.0) & within, parts[2 * i + 1], t)
    store(tg, t)
    parts = [part if within is None else jnp.where(within, part, parts[0]) for part, within in zip(parts, inside)]
    old = load(mx)
    if first is not None:
        old = jnp.where(first, parts[0], old)
    new = functools.reduce(jnp.maximum, parts, old)
    gap = old - new
    scale = jnp.exp(gap)
    s = load(sm)
    total = s * scale
    ent = (load(en) + gap * s) * scale
    for part, within in zip(parts, inside):
        d = part - new
        e = jnp.exp(d)
        if within is not None:
            e = jnp.where(within, e, 0.0)
        total += e
        ent += e * d
    store(mx, new)
    store(sm, total)
    store(en, ent)


def aim_rows(tok, tb, row0, count):
    ids = tok[pl.ds(row0, count), pl.ds(D - 64, 128)].astype(jnp.float32)
    value = ids[:, 64:65] * 256.0 + ids[:, 65:66]
    lane = lax.broadcasted_iota(jnp.int32, (count, 128), 1).astype(jnp.float32)
    tb[pl.ds(row0, count), :] = value - lane


def block_stats(mx, sm, en, tg, stats, block):
    rows = pl.ds(block * ROWS, ROWS)
    m, s, e = mx[rows, :].T, sm[rows, :].T, en[rows, :].T
    top = jnp.max(m, axis=0, keepdims=True)
    gap = m - top
    scale = jnp.exp(gap)
    stats[block, 0:1, :] = top
    stats[block, 1:2, :] = jnp.sum(s * scale, axis=0, keepdims=True)
    stats[block, 2:3, :] = jnp.sum((e + gap * s) * scale, axis=0, keepdims=True)
    stats[block, 3:4, :] = jnp.sum(tg[rows, :].T, axis=0, keepdims=True)


def norm_rows(hid, gain_ref, target_ref, stage):
    total = jnp.zeros((8, ROWS), jnp.float32)
    for i in range(0, D, 160):
        part = hid[i:i + 160, :].astype(jnp.float32)
        total += jnp.sum((part * part).reshape(20, 8, ROWS), axis=0)
    scale = lax.rsqrt(jnp.sum(total, axis=0, keepdims=True) * (1.0 / D) + EPS)
    target = target_ref[...]
    for i in range(0, DE, 128):
        if i + 128 <= D:
            part = hid[i:i + 128, :].astype(jnp.float32) * scale
            gain = gain_ref[:, i:i + 128].astype(jnp.float32)
            stage[:, i:i + 128] = (part.T * gain).astype(jnp.bfloat16)
        else:
            n = D - i
            part = hid[i:D, :].astype(jnp.float32) * scale
            row = lax.broadcasted_iota(jnp.int32, (128 - n, ROWS), 0)
            high = jnp.broadcast_to((target // 256).astype(jnp.float32), row.shape)
            low = jnp.broadcast_to((target % 256).astype(jnp.float32), row.shape)
            more = jnp.where(row == 0, high, jnp.where(row == 1, low, 0.0))
            gain = jnp.concatenate(
                [gain_ref[:, i:D].astype(jnp.float32), jnp.ones((1, 128 - n), jnp.float32)], axis=1
            )
            stage[:, i:i + 128] = (jnp.concatenate([part, more], axis=0).T * gain).astype(jnp.bfloat16)


def kernel(
    hid_ref, gain_ref, target_ref, head_ref, out_ref,
    hid, stage, tail, stage7, tok, hb, tb, mx, sm, en, tg, stats, inbox,
    load_sem, xs, xr, ys, yr, zs, zr, bs, br, ss, sr,
):
    tp, dp = lax.axis_index("tp"), lax.axis_index("dp")
    x, z = tp // NZ, tp % NZ
    y, core = dp // 2, dp % 2
    h = y % 2

    def x_peer(step):
        return {"tp": ((x + step) % NX) * NZ + z, "dp": dp}

    def y_peer(step):
        return {"tp": tp, "dp": ((y + step) % NY) * 2 + core}

    def z_peer(step):
        return {"tp": x * NZ + (z + step) % NZ, "dp": dp}

    twin = {"tp": tp, "dp": y * 2 + 1 - core}

    def remote(src, dst, send, recv, peer):
        return pltpu.make_async_remote_copy(
            src_ref=src, dst_ref=dst, send_sem=send, recv_sem=recv, device_id=peer, device_id_type=MESH
        )

    barrier = pltpu.get_barrier_semaphore()
    peers = [z_peer(d) for d in (4, 3, 5, 2, 6, 1, 7)] + [x_peer(1), x_peer(-1), y_peer(1), y_peer(-1), twin]
    for peer in peers:
        pl.semaphore_signal(barrier, inc=1, device_id=peer, device_id_type=MESH)

    own = PLACE[0] * ROWS
    hid_load = pltpu.make_async_copy(hid_ref, hid, load_sem.at[8])
    tail_load = pltpu.make_async_copy(head_ref.at[:, pl.ds((TILES - 1) * 128, LAST)], tail, load_sem.at[7])
    tile_loads = [
        pltpu.make_async_copy(head_ref.at[:, pl.ds(t * 128, 128)], hb.at[0, t], load_sem.at[t]) for t in range(TILES - 1)
    ]
    for copy in [hid_load, tail_load] + tile_loads:
        copy.start()

    sent = []

    def go(make):
        make().start()
        sent.append(make)

    def piece(shard, tile, sub):
        return hb.at[shard, tile, pl.ds(sub * SUB, SUB), :]

    def place(d, half):
        return tok.at[pl.ds(PLACE[d] * ROWS + half * HALF, HALF), :]

    def x_copy(side, i, src_shard):
        shard, quarter, sub = X_SEQ[side][i]
        tile = (2 * h + quarter) * 2 + core
        return remote(
            piece(src_shard, tile, sub), piece(shard, tile, sub), xs.at[side, i], xr.at[side, i],
            x_peer(-1 if side == 0 else 1),
        )

    def y_copy(side, i, parity):
        shard, quarter, sub = Y_SEQ[side][i]
        tile = (2 * parity + quarter) * 2 + core
        return remote(
            piece(shard, tile, sub), piece(shard, tile, sub), ys.at[side, i], yr.at[side, i],
            y_peer(-1 if side == 0 else 1),
        )

    def b_copy(kind, i, sender):
        shard, quarter, sub = (X_SEQ + Y_SEQ)[kind][i]
        parity = h if kind < 2 else 1 - h
        tile = (2 * parity + quarter) * 2 + sender
        return remote(piece(shard, tile, sub), piece(shard, tile, sub), bs.at[kind, i], br.at[kind, i], twin)

    def z_copy(side, i, src):
        d, half = Z_SEQ[side][i]
        return remote(
            place(src, half), place(d, half), zs.at[side, i], zr.at[side, i], z_peer(-1 if side == 0 else 1)
        )

    hid_load.wait()
    norm_rows(hid, gain_ref, target_ref, stage)
    tail_load.wait()
    stage7[...] = jnp.concatenate([tail[...], jnp.zeros((D, 128 - LAST), jnp.bfloat16)], axis=1)
    stage_copy = pltpu.make_async_copy(stage, tok.at[pl.ds(own, ROWS), :], load_sem.at[8])
    stage7_copy = pltpu.make_async_copy(stage7, hb.at[0, TILES - 1], load_sem.at[7])
    stage_copy.start()
    stage7_copy.start()
    pl.semaphore_wait(barrier, len(peers))
    stage_copy.wait()
    for i in range(2):
        for side in range(2):
            go(functools.partial(z_copy, side, i, 0))
    for copy in tile_loads:
        copy.wait()
    stage7_copy.wait()
    for i in range(2 * SUBS):
        for side in range(2):
            go(functools.partial(x_copy, side, i, 0))

    def zero(i, carry):
        rows = pl.ds(pl.multiple_of(i * ROWS, ROWS), ROWS)
        for ref in (mx, sm, en, tg):
            ref[rows, :] = jnp.zeros((ROWS, 128), jnp.float32)
        return carry

    lax.fori_loop(0, NZ, zero, 0)
    aim_rows(tok, tb, own, ROWS)

    def got_x(i):
        for side in range(2):
            shard, quarter, sub = X_SEQ[side][i]
            x_copy(side, i, 0).wait_recv()
            go(functools.partial(y_copy, quarter, Y_SEQ[quarter].index((shard, quarter, sub)), h))
            go(functools.partial(b_copy, side, i, core))
            if i < SUBS:
                go(functools.partial(x_copy, side, i + 2 * SUBS, shard))

    def got_y(i):
        for side in range(2):
            y_copy(side, i, 1 - h).wait_recv()
            go(functools.partial(b_copy, 2 + side, i, core))

    def got_tx(i):
        for kind in (0, 1):
            b_copy(kind, i, 1 - core).wait_recv()

    def got_ty(i):
        for kind in (2, 3):
            b_copy(kind, i, 1 - core).wait_recv()

    def got_z(i):
        for side in range(2):
            d, half = Z_SEQ[side][i]
            z_copy(side, i, 0).wait_recv()
            later = i + 2 if i < 4 else 6
            if i < 6 and Z_SEQ[side][later][1] == half:
                go(functools.partial(z_copy, side, later, d))
            aim_rows(tok, tb, PLACE[d] * ROWS + half * HALF, HALF)

    handlers = {"x": got_x, "y": got_y, "tx": got_tx, "ty": got_ty, "z": got_z}
    distance = {at: d for d, at in PLACE.items()}

    def figures_copy(block):
        d = distance[block]
        return remote(stats.at[block], inbox.at[NZ - d], ss.at[d], sr.at[NZ - d], z_peer(d))

    ahead, rest = plan()
    acts = [[functools.partial(handlers[kind], i) for kind, i in events] for events in ahead]
    acts.append([functools.partial(handlers[kind], i) for kind, i in rest])
    for step, blocks in DONE.items():
        for block in blocks:
            acts[step + 1].append(functools.partial(block_stats, mx, sm, en, tg, stats, block))
            acts[min(step + 2, len(STEPS))].append(functools.partial(go, functools.partial(figures_copy, block)))

    def run(i, low, high):
        if not any(acts[low:high]):
            return
        if high - low == 1:
            for act in acts[low]:
                act()
            return
        middle = (low + high) // 2
        if any(acts[low:middle]):
            pl.when(i < middle)(lambda: run(i, low, middle))
        if any(acts[middle:high]):
            pl.when(i >= middle)(lambda: run(i, middle, high))

    def columns_of(pairs):
        units = []
        for p in pairs:
            for shard, k in pair_units(p, h):
                step = jnp.where(shard == 2, 3, jnp.where(shard == 3, 2, shard))
                units.append((shard, k, (((x + step) % NX) * NZ + z) * WIDTH + k * 256))
        return units

    def one(i, carry):
        run(i, 0, len(STEPS))
        kind, rows, columns = packed(i)

        @pl.when(kind == 0)
        def _():
            base = 256 * ((rows - 1) // 2) + HALF * ((rows - 1) % 2)
            low = jnp.where(rows == 0, own, jnp.where(rows == 7, PLACE[4] * ROWS, base))
            step = jnp.where((rows == 0) | (rows == 7), HALF, ROWS)
            spans = [pl.ds(pl.multiple_of(low + j * step, HALF), HALF) for j in range(2)]
            pairs = [jnp.int32(QUADS[0][j]) for j in range(2)]
            for q in range(1, 4):
                pairs = [jnp.where(columns == q, QUADS[q][j], pairs[j]) for j in range(2)]
            compute_step(tok, hb, tb, mx, sm, en, tg, spans, columns_of(pairs), columns == 0)

        @pl.when(kind == 1)
        def _():
            spans = [pl.ds(pl.multiple_of(rows * 256, 256), 256)]
            compute_step(tok, hb, tb, mx, sm, en, tg, spans, columns_of([columns]), None)

        return carry

    lax.fori_loop(0, len(STEPS), one, 0)
    for act in acts[len(STEPS)]:
        act()
    block_stats(mx, sm, en, tg, stats, PLACE[0])
    for d in range(1, NZ):
        remote(stats.at[0], inbox.at[d], ss.at[d], sr.at[d], z_peer(d)).wait_recv()
    all_of = [stats[PLACE[0]]] + [inbox[d] for d in range(1, NZ)]
    top = functools.reduce(jnp.maximum, [part[0:1, :] for part in all_of])
    total = ent = tgt = jnp.zeros((1, ROWS), jnp.float32)
    for part in all_of:
        gap = part[0:1, :] - top
        scale = jnp.exp(gap)
        total += part[1:2, :] * scale
        ent += (part[2:3, :] + gap * part[1:2, :]) * scale
        tgt += part[3:4, :]
    log_total = jnp.log(total)
    out_ref[0:1, :] = tgt - (top + log_total)
    out_ref[1:2, :] = log_total - ent / total
    for make in sent:
        make().wait_send()


def on_device(hidden, gain, head, lengths, mask, targets):
    rows = hidden.shape[0]
    me = lax.axis_index("tp")
    vm = pltpu.VMEM
    dma = pltpu.SemaphoreType.DMA
    stat = vm((NZ * ROWS, 128), jnp.float32)
    small = vm((NZ, 8, 128), jnp.float32)
    anywhere, near = pl.BlockSpec(memory_space=pl.ANY), pl.BlockSpec(memory_space=pltpu.VMEM)
    out = pl.pallas_call(
        kernel,
        out_shape=jax.ShapeDtypeStruct((8, ROWS), jnp.float32),
        in_specs=[anywhere, near, near, anywhere],
        out_specs=near,
        scratch_shapes=[
            vm((D, ROWS), jnp.bfloat16),
            vm((ROWS, DE), jnp.bfloat16),
            vm((D, LAST), jnp.bfloat16),
            vm((D, 128), jnp.bfloat16),
            vm((NZ * ROWS, DE), jnp.bfloat16),
            vm((NX, TILES, D, 128), jnp.bfloat16),
            stat, stat, stat, stat, stat,
            small, small,
            dma((9,)),
            dma((2, 3 * SUBS)), dma((2, 3 * SUBS)),
            dma((2, 3 * SUBS)), dma((2, 3 * SUBS)),
            dma((2, 7)), dma((2, 7)),
            dma((4, 3 * SUBS)), dma((4, 3 * SUBS)),
            dma((NZ,)), dma((NZ,)),
        ],
        compiler_params=pltpu.CompilerParams(
            collective_id=0, has_side_effects=True, vmem_limit_bytes=62 << 20
        ),
    )(hidden.T, gain.reshape(1, D), targets.reshape(1, rows), head)
    row_ids = me * rows + jnp.arange(rows, dtype=jnp.int32)
    slot = row_ids % SEQ_LEN
    seq_id = row_ids // SEQ_LEN
    match = seq_id[:, None] == jnp.arange(lengths.shape[0], dtype=jnp.int32)[None, :]
    seq_len = jnp.sum(jnp.where(match, lengths[None, :], 0), axis=1)
    valid = (slot < seq_len) & (mask == 1)
    return (jnp.where(valid, out[0], 0.0), jnp.where(valid, out[1], 0.0))


def solution(mesh):
    return jax.shard_map(
        on_device,
        mesh=mesh,
        in_specs=(
            P(("dp", "tp"), None),
            P(),
            P(None, "tp"),
            P("dp"),
            P(("dp", "tp")),
            P(("dp", "tp")),
        ),
        out_specs=(P(("dp", "tp")), P(("dp", "tp"))),
        check_vma=False,
    )
```
